32 devices in a mesh: ctx: 8 (over z, x), tp: 4 (over y, core).
Axes of the slice: x: 2, y: 2, z: 4, core: 2. Of those that a mesh axis runs over, the one named last changes fastest.
Arguments:
- residual: bfloat16 [1024, 4096], P('ctx', 'tp')
- mixer_input: bfloat16 [1024, 4096], P('ctx', 'tp')
- gate_input: bfloat16 [1024, 4096], P('ctx', 'tp'), may hold values from -6 to 6
- state_proj: bfloat16 [1024, 32], P('ctx'), may hold values from -6 to 6
- step_raw: float32 [1024, 64], P('ctx', 'tp'), may hold values from -5 to 5
- conv_weight: float32 [4, 4096], P(None, 'tp'), may hold values from -3 to 3
- conv_state_weight: float32 [4, 32], replicated, may hold values from -3 to 3
- step_bias: float32 [64], P('tp'), may hold values from -3.5 to 0.5
- decay_log: float32 [64], P('tp')
- skip_gain: float32 [64], P('tp'), may hold values from 0.5 to 1.5
- mixer_gain: float32 [4096], P('tp'), may hold values from 0.5 to 1.5
- out_weight: bfloat16 [4096, 4096], P('tp', 'ctx'), may hold values from -0.09375 to 0.09375
- feed_gain: float32 [4096], P('tp'), may hold values from 0.5 to 1.5
- expert_gate: bfloat16 [8, 4096, 7168], P('ctx', 'tp'), may hold values from -0.09375 to 0.09375
- expert_up: bfloat16 [8, 4096, 7168], P('ctx', 'tp'), may hold values from -0.09375 to 0.09375
- expert_down: bfloat16 [8, 7168, 4096], P('ctx', None, 'tp'), may hold values from -0.0625 to 0.0625
- expert_ids: int32 [1024, 2], P('ctx'), may hold values from 0 to 7, all different within a row; in each aligned block of 128 rows (0 to 127, 128 to 255, ...) at most 36 rows name the same one
- expert_weights: float32 [1024, 2], P('ctx'), may hold values from 0.1 to 0.9
Outputs:
- block_out: bfloat16 [1024, 4096], P('ctx', 'tp')
The draws below stay inside these ranges and needn't reach their ends.
Inputs may be any that keep to these rules, and one draw needn't show every extreme that they name: `expert_ids`: in each aligned block of 128 rows no expert is named more than 36 times, and some block reaches 36; the two experts of a row differ.
All inputs are finite; a program needn't handle non-finite values.
Results may differ from the reference program's by a relative error of at most 0.014.
Values may be sent and summed in bfloat16 or wider, within the bound.
A program may use at most 128 MiB of HBM per device.

```python
import math
import jax
import jax.numpy as jnp
import numpy as np
from jax import lax

D = 4096
E = 4096
HEADDIM = 64
NSTATE = 16
CONV = 4
EXPERTS = 8
TOPK = 2
FF = 7168
TOK_DEV = 128
HEADS = 64
CAP = 36
GROUP = 1
FFG = 7168
TOKENS = 1024
N_CTX = 8
N_TP = 4


def rising_field(key, rows, columns):
    first, second, third = jax.random.split(key, 3)
    base = jax.random.normal(first, (rows, columns), jnp.float32)
    ramp = jnp.exp(math.log(10.0) * jnp.arange(columns, dtype=jnp.float32) / columns)
    rough = jax.random.uniform(second, (columns,), jnp.float32, 0.6, 1.4)
    row_scale = jnp.exp(jax.random.uniform(third, (rows, 1), jnp.float32, -0.7, 0.7))
    return base * (ramp * rough / 4.0)[None, :] * row_scale


def draw_residual(key, part):
    return rising_field(jax.random.fold_in(key, 3), TOKENS, D).astype(jnp.bfloat16)


def draw_mixer_input(key, part):
    return rising_field(jax.random.fold_in(key, 5), TOKENS, E).astype(jnp.bfloat16)


def head_plan(key):
    base = jax.random.fold_in(key, 17)
    first, second, third = jax.random.split(base, 3)
    share = 0.5
    slow = jax.random.uniform(first, (HEADS,), jnp.float32) < share
    offset = jax.random.uniform(second, (HEADS,), jnp.float32, -1.0, 1.0)
    spread = jax.random.uniform(third, (HEADS,), jnp.float32, 0.0, 1.0)
    return (slow, offset, spread)


def draw_step_bias(key, part):
    slow, offset, spread = head_plan(key)
    return jnp.where(slow, -3.0 + 0.5 * offset, 0.5 * offset).astype(jnp.float32)


def draw_decay_log(key, part):
    slow, offset, spread = head_plan(key)
    fast_rate = math.log(1.0 / 50.0) + spread * math.log(50.0 / 30.0) - math.log(0.8)
    slow_rate = math.log(0.3) + spread * math.log(5.0) - math.log(0.07) - jnp.log(jnp.float32(TOKENS))
    return jnp.where(slow, slow_rate, fast_rate).astype(jnp.float32)


def block_levels(own_key, dims, cuts, least, largest):
    gain, own = 1.0, jax.random.fold_in(own_key, 6)
    for dim, shards_of in cuts:
        heights = jnp.exp(jax.random.uniform(jax.random.fold_in(own, dim), (shards_of,), jnp.float32, least / len(cuts), largest / len(cuts)))
        gain = gain * jnp.repeat(heights, dims[dim] // shards_of).reshape([-1 if axis == dim else 1 for axis in range(len(dims))])
    return gain


def shared_out(stream_key, own, number, rows, count, top, bound, slope):
    sequence = jax.random.permutation(stream_key, count)
    packed, usual = portions_of(count, rows * top, bound, slope, True), portions_of(count, rows * top, bound, slope, False)
    places = jnp.arange(count)

    def named(lengths, offset_by):
        used = int((lengths > 0).sum())
        fixed = max(1, used // 4)
        passed = fixed + (places - fixed + offset_by * (used - fixed)) % max(1, count - fixed)
        return jnp.zeros((count,), jnp.int32).at[sequence[jnp.where(places < fixed, places, passed)]].set(jnp.asarray(lengths, jnp.int32))

    lengths = jnp.where(number % 4 == 0, named(packed, number // 4), named(usual, number - number // 4 - 1))
    mixed = jax.random.permutation(jax.random.fold_in(own, 3), count)
    giver, sink = mixed[0:count // 2 * 2:2], mixed[1:count // 2 * 2:2]
    room = jnp.minimum(lengths[giver] - 1, bound - lengths[sink]) // 2
    room = jnp.where((giver == sequence[0]) | (sink == sequence[0]) | (lengths[sink] == 0), 0, jnp.maximum(room, 0))
    passed = jax.random.randint(jax.random.fold_in(own, 4), (count // 2,), 0, 1 << 20) % (room + 1)
    lengths = lengths.at[giver].add(-passed).at[sink].add(passed)
    labels = jnp.searchsorted(jnp.cumsum(lengths), jnp.arange(rows * top), side="right").astype(jnp.int32)
    grid = labels.reshape(top, rows).T
    grid = grid[jax.random.permutation(jax.random.fold_in(own, 1), rows)]
    offset_by = jax.random.randint(jax.random.fold_in(own, 2), (rows, 1), 0, top)
    return jnp.take_along_axis(grid, (jnp.arange(top)[None, :] + offset_by) % top, axis=1)


def portions_of(amount, total, bound, lean, full):
    portions = [(1 << 20) // math.isqrt(grade ** lean) + 1 for grade in range(1, amount + 1)]
    largest = bound if full else min(bound, max(-(-total // amount), total * portions[0] // sum(portions)))
    least = 1 if total - largest >= amount - 1 else 0
    given, rest = [largest] + [least] * (amount - 1), total - largest - least * (amount - 1)
    while rest > 0:
        free = [i for i in range(1, amount) if given[i] < largest] or [i for i in range(1, amount) if given[i] < bound]
        whole, budget = sum([portions[i] for i in free]), rest
        for i in free:
            more = min(bound - given[i], max(1, budget * portions[i] // whole), rest)
            given[i] = given[i] + more
            rest = rest - more
    return np.array(given)


def noise(rng, shape, scale, bound, cuts=(), kind=jnp.bfloat16):
    drawn = jax.random.normal(rng, shape, jnp.float32) * scale
    if len(cuts) > 0:
        drawn = block_levels(rng, shape, cuts, -0.22, 0.18) * drawn
    return jnp.clip(drawn, min=-bound, max=bound).astype(kind)


def setup_inputs(seed: int = 0) -> dict:
    splits = jax.random.split(jax.random.key(seed), 19)
    residual = draw_residual(jax.random.fold_in(splits[18], 71), 0)
    mixer_input = draw_mixer_input(jax.random.fold_in(splits[18], 71), 0)
    gate_input = noise(splits[2], (TOKENS, E), 1.0, 6.0, ((0, 8), (1, 4)))
    state_proj = noise(splits[3], (TOKENS, 2 * NSTATE), 1.0, 6.0, ((0, 8),))
    step_raw = noise(splits[4], (TOKENS, HEADS), 1.0, 5.0, ((0, 8), (1, 4)), jnp.float32)
    conv_weight = noise(splits[5], (CONV, E), CONV ** -0.5, 3.0, ((1, 4),), jnp.float32)
    conv_state_weight = noise(splits[6], (CONV, 2 * NSTATE), CONV ** -0.5, 3.0, (), jnp.float32)
    step_bias = draw_step_bias(jax.random.fold_in(splits[18], 71), 0)
    decay_log = draw_decay_log(jax.random.fold_in(splits[18], 71), 0)
    skip_gain = jnp.clip(0.5 + 1.0 * jax.random.uniform(splits[9], (HEADS,), jnp.float32) ** block_levels(splits[9], (HEADS,), ((0, 4),), -0.2, 0.2), 0.5, 1.5)
    mixer_gain = jnp.clip(1.0 + 0.1 * jax.random.normal(splits[10], (E,), jnp.float32), 0.5, 1.5)
    out_weight = noise(splits[11], (E, D), E ** -0.5, 0.09375, ((0, 4), (1, 8)))
    feed_gain = jnp.clip(1.0 + 0.1 * jax.random.normal(splits[12], (D,), jnp.float32), 0.5, 1.5)
    expert_gate = noise(splits[13], (EXPERTS * GROUP, D, FFG), D ** -0.5, 0.09375, ((0, 8), (1, 4)))
    expert_up = noise(splits[14], (EXPERTS * GROUP, D, FFG), D ** -0.5, 0.09375, ((0, 8), (1, 4)))
    expert_down = noise(splits[15], (EXPERTS * GROUP, FFG, D), FF ** -0.5, 0.0625, ((0, 8), (2, 4)))
    expert_ids_keys = jax.random.split(jax.random.fold_in(splits[16], 1), TOKENS // TOK_DEV)
    expert_ids_turns = jax.random.permutation(jax.random.fold_in(splits[16], 3), TOKENS // TOK_DEV)
    expert_ids = jax.vmap(lambda own, number: shared_out(jax.random.fold_in(splits[16], 2), own, number, TOK_DEV, EXPERTS, TOPK, CAP, 2))(expert_ids_keys, expert_ids_turns).reshape((TOKENS, TOPK))
    expert_weights = jnp.clip(0.1 + 0.79999997 * jax.random.uniform(splits[17], (TOKENS, TOPK), jnp.float32) ** block_levels(splits[17], (TOKENS, TOPK), ((0, 8),), -0.2, 0.2), 0.1, 0.9)
    return dict(residual=residual, mixer_input=mixer_input, gate_input=gate_input, state_proj=state_proj, step_raw=step_raw, conv_weight=conv_weight, conv_state_weight=conv_state_weight, step_bias=step_bias, decay_log=decay_log, skip_gain=skip_gain, mixer_gain=mixer_gain, out_weight=out_weight, feed_gain=feed_gain, expert_gate=expert_gate, expert_up=expert_up, expert_down=expert_down, expert_ids=expert_ids, expert_weights=expert_weights)


EPSILON = 1e-05

def causal_filter(previous, current, kernel):
    joined = jnp.concatenate([previous, current], axis=0)
    length = current.shape[0]
    total = jnp.zeros(current.shape, jnp.float32)
    for offset in range(kernel.shape[0]):
        total = total + kernel[offset][None, :] * joined[offset:offset + length]
    return jax.nn.silu(total)

def local_terms(values, writer, reader, step_size, log_decay):
    length = values.shape[0]
    cumulative = jnp.cumsum(log_decay, axis=0)
    scores = jnp.dot(reader, writer.T, precision=lax.Precision.HIGHEST)
    order = jnp.arange(length)
    causal = (order[:, None] >= order[None, :])[:, :, None]
    spans = cumulative[:, None, :] - cumulative[None, :, :]
    factor = jnp.where(causal, jnp.exp(jnp.where(causal, spans, 0.0)), 0.0)
    factor = factor * step_size[None, :, :] * scores[:, :, None]
    inside = jnp.einsum('tsh,shp->thp', factor, values, precision=lax.Precision.HIGHEST)
    tail = cumulative[length - 1]
    ending = jnp.exp(tail[None, :] - cumulative) * step_size
    fresh = jnp.einsum('th,thp,tn->hpn', ending, values, writer, precision=lax.Precision.HIGHEST)
    return (inside, cumulative, fresh, tail)

def expert_rows(rows, gate_block, up_block, down_block):
    count = rows.shape[0]
    split_rows = rows.reshape(count, N_TP, D // N_TP).astype(jnp.float32)
    gate_split = gate_block.reshape(GROUP, N_TP, D // N_TP, FFG).astype(jnp.float32)
    up_split = up_block.reshape(GROUP, N_TP, D // N_TP, FFG).astype(jnp.float32)
    gate_terms = jnp.einsum('rtd,gtdf->tgrf', split_rows, gate_split, precision=lax.Precision.HIGHEST)
    up_terms = jnp.einsum('rtd,gtdf->tgrf', split_rows, up_split, precision=lax.Precision.HIGHEST)
    gate_sum = lax.optimization_barrier(jnp.sum(lax.optimization_barrier(gate_terms.astype(jnp.bfloat16)).astype(jnp.float32), axis=0))
    up_sum = lax.optimization_barrier(jnp.sum(lax.optimization_barrier(up_terms.astype(jnp.bfloat16)).astype(jnp.float32), axis=0))
    activated = (jax.nn.silu(gate_sum) * up_sum).astype(jnp.bfloat16)
    activated_wide = lax.optimization_barrier(activated).astype(jnp.float32)
    pieces = jnp.einsum('grf,gfd->grd', activated_wide, down_block.astype(jnp.float32), precision=lax.Precision.HIGHEST)
    return lax.optimization_barrier(jnp.sum(lax.optimization_barrier(pieces.astype(jnp.bfloat16)).astype(jnp.float32), axis=0))

def reference(residual, mixer_input, gate_input, state_proj, step_raw, conv_weight, conv_state_weight, step_bias, decay_log, skip_gain, mixer_gain, out_weight, feed_gain, expert_gate, expert_up, expert_down, expert_ids, expert_weights):
    joined = jnp.concatenate([mixer_input, state_proj], axis=1).astype(jnp.float32)
    kernel = jnp.concatenate([conv_weight, conv_state_weight], axis=1)
    previous = jnp.zeros((CONV - 1, joined.shape[1]), jnp.float32)
    filtered = causal_filter(previous, joined, kernel)
    values = filtered[:, :E].reshape(N_CTX, TOK_DEV, HEADS, HEADDIM)
    writer = filtered[:, E:E + NSTATE].reshape(N_CTX, TOK_DEV, NSTATE)
    reader = filtered[:, E + NSTATE:].reshape(N_CTX, TOK_DEV, NSTATE)
    step_flat = jax.nn.softplus(step_raw + step_bias[None, :])
    log_decay = (-step_flat * jnp.exp(decay_log)[None, :]).reshape(N_CTX, TOK_DEV, HEADS)
    step_size = step_flat.reshape(N_CTX, TOK_DEV, HEADS)

    def advance(state, block):
        values_block, writer_block, reader_block, size_block, decay_block = block
        inside, cumulative, fresh, tail = local_terms(values_block, writer_block, reader_block, size_block, decay_block)
        carried = jnp.einsum('tn,hpn->thp', reader_block, state, precision=lax.Precision.HIGHEST) * jnp.exp(cumulative)[:, :, None]
        mixed_block = inside + carried + skip_gain[None, :, None] * values_block
        return (jnp.exp(tail)[:, None, None] * state + fresh, mixed_block)
    start = jnp.zeros((HEADS, HEADDIM, NSTATE), jnp.float32)
    final_state, mixed = lax.scan(advance, start, (values, writer, reader, step_size, log_decay))
    gated = mixed.reshape(TOKENS, E) * jax.nn.silu(gate_input.astype(jnp.float32))
    scale = lax.rsqrt(lax.optimization_barrier(jnp.mean(gated * gated, axis=1)) + EPSILON)
    normed = (gated * scale[:, None] * mixer_gain[None, :]).astype(jnp.bfloat16)
    mixer_out = jnp.dot(normed, out_weight, preferred_element_type=jnp.float32)
    hidden_state = (residual.astype(jnp.float32) + mixer_out).astype(jnp.bfloat16)
    state_float = lax.optimization_barrier(hidden_state).astype(jnp.float32)
    norm_scale = lax.rsqrt(lax.optimization_barrier(jnp.mean(state_float * state_float, axis=1)) + EPSILON)
    expert_input = (state_float * norm_scale[:, None] * feed_gain[None, :]).astype(jnp.bfloat16)
    blocks = expert_ids.reshape(N_CTX, TOK_DEV * TOPK).astype(jnp.int32)
    matches = (blocks[:, :, None] == jnp.arange(EXPERTS, dtype=jnp.int32)[None, None, :]).astype(jnp.int32)
    slots = lax.optimization_barrier(jnp.sum((jnp.cumsum(matches, axis=1) - matches) * matches, axis=2)).astype(jnp.int32)
    targets = (blocks * CAP + slots).astype(jnp.int32)
    rows = jnp.repeat(expert_input.reshape(N_CTX, TOK_DEV, D), TOPK, axis=1)
    owners = jnp.arange(N_CTX, dtype=jnp.int32)[:, None]
    buffer = jnp.zeros((N_CTX, EXPERTS * CAP, D), jnp.bfloat16).at[owners, targets].set(rows)
    gate_all = expert_gate.reshape(EXPERTS, GROUP, D, FFG)
    up_all = expert_up.reshape(EXPERTS, GROUP, D, FFG)
    down_all = expert_down.reshape(EXPERTS, GROUP, FFG, D)

    def one_expert(index):
        picked = lax.dynamic_slice_in_dim(buffer, (index * CAP).astype(jnp.int32), CAP, 1).reshape(N_CTX * CAP, D)
        return expert_rows(picked, gate_all[index], up_all[index], down_all[index]).reshape(N_CTX, CAP, D)
    outputs = lax.map(one_expert, jnp.arange(EXPERTS, dtype=jnp.int32))
    chosen = outputs[blocks, owners, slots].reshape(TOKENS, TOPK, D)
    routed = lax.optimization_barrier(jnp.sum(expert_weights[:, :, None] * chosen, axis=1))
    return (state_float + routed).astype(jnp.bfloat16)
```

```python
import jax
import jax.numpy as jnp
from jax import lax
from jax.sharding import PartitionSpec as P

EXPERTS = 8
CAP = 36


EPSILON = 1e-05


def passed_along(value, axis, steps):
    count = lax.axis_size(axis)
    first, last = (max(0, -steps), min(count, count - steps))
    return lax.ppermute(value, axis, [(source, source + steps) for source in range(first, last)])


def swapped(value, distance):
    return lax.ppermute(value, "tp", [(p, p ^ distance) for p in range(lax.axis_size("tp"))])


def entering(decay, fresh, axis):
    peers, position = (lax.axis_size(axis), lax.axis_index(axis))
    packed = jnp.concatenate([fresh, decay[None, :]], axis=0).astype(jnp.bfloat16)
    everything = lax.all_gather(packed, axis).astype(jnp.float32)

    def step(k, before):
        part = everything[k]
        return jnp.where(k < position, part[-1:] * before + part[:-1], before)

    return lax.fori_loop(0, peers, step, jnp.zeros_like(fresh))


def causal_filter(previous, current, kernel):
    joined = jnp.concatenate([previous, current], axis=0)
    length = current.shape[0]
    total = jnp.zeros(current.shape, jnp.float32)
    for offset in range(kernel.shape[0]):
        total = total + kernel[offset][None, :] * joined[offset : offset + length]
    return jax.nn.silu(total)


def local_terms(values, writer, reader, step_size, log_decay):
    length = values.shape[0]
    cumulative = jnp.cumsum(log_decay, axis=0)
    scores = jnp.dot(reader, writer.T, precision=lax.Precision.HIGHEST)
    order = jnp.arange(length)
    causal = (order[:, None] >= order[None, :])[:, :, None]
    spans = cumulative[:, None, :] - cumulative[None, :, :]
    factor = jnp.where(causal, jnp.exp(jnp.where(causal, spans, 0.0)), 0.0)
    factor = factor * step_size[None, :, :] * scores[:, :, None]
    inside = jnp.einsum("tsh,shp->thp", factor, values, precision=lax.Precision.HIGHEST)
    tail = cumulative[length - 1]
    ending = jnp.exp(tail[None, :] - cumulative) * step_size
    weighted = (ending[:, :, None] * values).reshape(length, -1)
    fresh = jnp.dot(writer.T, weighted, precision=lax.Precision.HIGHEST)
    return (inside, cumulative, fresh, tail)


def body(
    residual,
    mixer_input,
    gate_input,
    state_proj,
    step_raw,
    conv_weight,
    conv_state_weight,
    step_bias,
    decay_log,
    skip_gain,
    mixer_gain,
    out_weight,
    feed_gain,
    expert_gate,
    expert_up,
    expert_down,
    expert_ids,
    expert_weights,
):
    tensor_count = lax.axis_size("tp")
    context_count = lax.axis_size("ctx")
    tokens = mixer_input.shape[0]
    channels = mixer_input.shape[1]
    states = state_proj.shape[1] // 2
    heads_local = step_raw.shape[1]
    head_size = channels // heads_local
    taps = conv_weight.shape[0]
    joined = jnp.concatenate([mixer_input, state_proj], axis=1)
    previous = passed_along(joined[tokens - (taps - 1) :], "ctx", 1)
    kernel = jnp.concatenate([conv_weight, conv_state_weight], axis=1)
    filtered = causal_filter(previous.astype(jnp.float32), joined.astype(jnp.float32), kernel)
    values = filtered[:, :channels].reshape(tokens, heads_local, head_size)
    writer = filtered[:, channels : channels + states]
    reader = filtered[:, channels + states :]
    step_size = jax.nn.softplus(step_raw + step_bias[None, :])
    log_decay = -step_size * jnp.exp(decay_log)[None, :]
    inside, cumulative, fresh, tail = local_terms(values, writer, reader, step_size, log_decay)

    incoming = entering(jnp.repeat(jnp.exp(tail), head_size), fresh, "ctx")
    carried = (
        jnp.dot(reader, incoming, precision=lax.Precision.HIGHEST).reshape(values.shape)
        * jnp.exp(cumulative)[:, :, None]
    )
    mixed = inside + carried + skip_gain[None, :, None] * values
    gated = mixed.reshape(tokens, channels) * jax.nn.silu(gate_input.astype(jnp.float32))
    tp_index = lax.axis_index("tp")
    core, chip = (tp_index % 2, tp_index // 2)
    everyone = lax.all_gather(
        (gated * mixer_gain[None, :]).astype(jnp.bfloat16), "ctx", axis=0, tiled=True
    )
    square_sum = lax.psum(jnp.sum(gated * gated, axis=1), "tp")
    scale = lax.rsqrt(square_sum / (channels * tensor_count) + EPSILON)
    span = everyone.shape[0] // tensor_count

    def projected(quarter):
        rows = lax.dynamic_slice_in_dim(everyone, quarter * span, span, 0)
        return jnp.dot(rows, out_weight, preferred_element_type=jnp.float32)

    own, beside = (chip * 2 + core, chip * 2 + 1 - core)
    across, diagonal = ((1 - chip) * 2 + core, (1 - chip) * 2 + 1 - core)
    far = swapped(projected(diagonal).astype(jnp.bfloat16), 1)
    far = swapped((projected(across) + far.astype(jnp.float32)).astype(jnp.bfloat16), 2)
    near = swapped(projected(beside).astype(jnp.bfloat16), 1)
    reduced = projected(own) + near.astype(jnp.float32) + far.astype(jnp.float32)
    blocks = context_count // tensor_count
    reduced = reduced.astype(jnp.bfloat16).reshape(blocks, tokens, -1)
    ctx_index = lax.axis_index("ctx")
    pieces = []
    for j in range(blocks):
        moves = [
            (c * tensor_count + p, (p * blocks + (c + j) % blocks) * tensor_count + c // blocks)
            for c in range(context_count)
            for p in range(tensor_count)
        ]
        block = lax.dynamic_index_in_dim(reduced, (ctx_index + j) % blocks, 0, keepdims=False)
        pieces.append(lax.ppermute(block, ("ctx", "tp"), moves))
    stacked = jnp.stack(pieces)
    order = (ctx_index - jnp.arange(blocks)) % blocks
    if blocks == 2:
        first = ctx_index % 2 == 0
        mixer_out = jnp.concatenate(
            [jnp.where(first, pieces[0], pieces[1]), jnp.where(first, pieces[1], pieces[0])], axis=1
        )
    else:
        mixer_out = jnp.take(stacked, order, axis=0).transpose(1, 0, 2).reshape(tokens, -1)
    mixer_out = mixer_out.astype(jnp.float32) * scale[:, None]
    hidden_state = (residual.astype(jnp.float32) + mixer_out).astype(jnp.bfloat16)
    state_float = lax.optimization_barrier(hidden_state).astype(jnp.float32)
    width_total = hidden_state.shape[1] * tensor_count
    feed_sum = lax.psum(jnp.sum(state_float * state_float, axis=1), "tp")
    feed_scale = lax.rsqrt(feed_sum / width_total + EPSILON)
    expert_input = (state_float * feed_scale[:, None] * feed_gain[None, :]).astype(jnp.bfloat16)
    group = context_count // EXPERTS
    width_local = expert_input.shape[1]
    flat_experts = expert_ids.reshape(-1)
    matches = (flat_experts[:, None] == jnp.arange(EXPERTS)[None, :]).astype(jnp.int32)
    slots = jnp.sum((jnp.cumsum(matches, axis=0) - matches) * matches, axis=1)
    targets = (flat_experts * CAP + slots).reshape(tokens, -1)
    picker = jnp.any(targets[None, :, :] == jnp.arange(EXPERTS * CAP)[:, None, None], axis=2)
    buffer = jnp.dot(
        picker.astype(jnp.bfloat16), expert_input, preferred_element_type=jnp.float32
    ).astype(jnp.bfloat16)
    outgoing = jnp.broadcast_to(
        buffer.reshape(EXPERTS, 1, CAP, width_local), (EXPERTS, group, CAP, width_local)
    )
    outgoing = outgoing.reshape(EXPERTS * group, CAP, width_local)
    gate_local = expert_gate[0]
    up_local = expert_up[0]
    down_local = expert_down[0]
    arrived = lax.all_to_all(outgoing, "ctx", split_axis=0, concat_axis=0, tiled=True)
    sources, items, depth = arrived.shape
    flattened = arrived.reshape(sources * items, depth)
    hidden = gate_local.shape[1] // tensor_count

    def product(weight, quarter):
        columns = lax.dynamic_slice_in_dim(weight, quarter * hidden, hidden, 1)
        return jnp.dot(flattened, columns, preferred_element_type=jnp.float32)

    weights = (gate_local, up_local)
    fars = []
    for weight in weights:
        far = swapped(product(weight, diagonal).astype(jnp.bfloat16), 1)
        far = (product(weight, across) + far.astype(jnp.float32)).astype(jnp.bfloat16)
        fars.append(swapped(far, 2))
    nears = [swapped(product(weight, beside).astype(jnp.bfloat16), 1) for weight in weights]
    gate_share, up_share = (
        product(weight, own).astype(jnp.bfloat16).astype(jnp.float32)
        + near.astype(jnp.float32)
        + far.astype(jnp.float32)
        for weight, near, far in zip(weights, nears, fars)
    )
    share = (jax.nn.silu(gate_share) * up_share).astype(jnp.bfloat16)
    share_across = swapped(share, 2)
    share_beside = swapped(share, 1)
    share_diagonal = swapped(share_across, 1)

    def lowered(part, quarter):
        rows = lax.dynamic_slice_in_dim(down_local, quarter * hidden, hidden, 0)
        return jnp.dot(part, rows, preferred_element_type=jnp.float32)

    answer = (
        lowered(share, own)
        + lowered(share_beside, beside)
        + lowered(share_across, across)
        + lowered(share_diagonal, diagonal)
    ).astype(jnp.bfloat16)
    answers = lax.all_to_all(
        answer.reshape(sources, items, depth), "ctx", split_axis=0, concat_axis=0, tiled=True
    )
    summed = jnp.sum(answers.reshape(EXPERTS, group, CAP, width_local), axis=1, dtype=jnp.float32)
    summed = summed.reshape(EXPERTS * CAP, width_local)
    chosen = jnp.take(summed, targets, axis=0)
    routed = jnp.sum(expert_weights[:, :, None] * chosen, axis=1)
    return (state_float + routed).astype(jnp.bfloat16)


def solution(mesh):
    placed = (
        P("ctx", "tp"),
        P("ctx", "tp"),
        P("ctx", "tp"),
        P("ctx", None),
        P("ctx", "tp"),
        P(None, "tp"),
        P(),
        P("tp"),
        P("tp"),
        P("tp"),
        P("tp"),
        P("tp", "ctx"),
        P("tp"),
        P("ctx", "tp", None),
        P("ctx", "tp", None),
        P("ctx", None, "tp"),
        P("ctx", None),
        P("ctx", None),
    )
    return jax.shard_map(
        body, mesh=mesh, in_specs=placed, out_specs=P("ctx", "tp"), check_vma=False
    )
```

```python
import jax
import jax.numpy as jnp
from jax import lax
from jax.sharding import PartitionSpec as P

EXPERTS = 8
CAP = 36


EPSILON = 1e-05


def passed_along(value, axis, steps):
    count = lax.axis_size(axis)
    first, last = (max(0, -steps), min(count, count - steps))
    return lax.ppermute(value, axis, [(source, source + steps) for source in range(first, last)])


def swapped(value, distance):
    return lax.ppermute(value, "tp", [(p, p ^ distance) for p in range(lax.axis_size("tp"))])


def rotated(value, steps):
    count = lax.axis_size("ctx")
    return lax.ppermute(value, "ctx", [(c, (c + steps) % count) for c in range(count)])


def tensor_total(value):
    return (value + swapped(value, 1)) + (swapped(value, 2) + swapped(value, 3))


def entering(decay, fresh, axis):
    peers, position = (lax.axis_size(axis), lax.axis_index(axis))
    packed = jnp.concatenate([fresh, decay[None, :]], axis=0).astype(jnp.bfloat16)
    if peers == EXPERTS:
        total, carry = (jnp.zeros_like(fresh), jnp.ones_like(decay)[None, :])
        for distance in range(1, peers):
            part = passed_along(packed, axis, distance).astype(jnp.float32)
            total = total + carry * part[:-1]
            carry = carry * part[-1:]
        return total
    everything = lax.all_gather(packed, axis).astype(jnp.float32)

    def step(k, before):
        part = everything[k]
        return jnp.where(k < position, part[-1:] * before + part[:-1], before)

    return lax.fori_loop(0, peers, step, jnp.zeros_like(fresh))


def causal_filter(previous, current, kernel):
    joined = jnp.concatenate([previous, current], axis=0)
    length = current.shape[0]
    total = jnp.zeros(current.shape, jnp.float32)
    for offset in range(kernel.shape[0]):
        total = total + kernel[offset][None, :] * joined[offset : offset + length]
    return jax.nn.silu(total)


def local_terms(values, writer, reader, step_size, log_decay):
    length = values.shape[0]
    cumulative = jnp.cumsum(log_decay, axis=0)
    scores = jnp.dot(reader, writer.T, precision=lax.Precision.HIGHEST)
    order = jnp.arange(length)
    causal = (order[:, None] >= order[None, :])[:, :, None]
    spans = cumulative[:, None, :] - cumulative[None, :, :]
    factor = jnp.where(causal, jnp.exp(jnp.where(causal, spans, 0.0)), 0.0)
    factor = factor * step_size[None, :, :] * scores[:, :, None]
    inside = jnp.einsum("tsh,shp->thp", factor, values, precision=lax.Precision.HIGHEST)
    tail = cumulative[length - 1]
    ending = jnp.exp(tail[None, :] - cumulative) * step_size
    weighted = (ending[:, :, None] * values).reshape(length, -1)
    fresh = jnp.dot(writer.T, weighted, precision=lax.Precision.HIGHEST)
    return (inside, cumulative, fresh, tail)


def body(
    residual,
    mixer_input,
    gate_input,
    state_proj,
    step_raw,
    conv_weight,
    conv_state_weight,
    step_bias,
    decay_log,
    skip_gain,
    mixer_gain,
    out_weight,
    feed_gain,
    expert_gate,
    expert_up,
    expert_down,
    expert_ids,
    expert_weights,
):
    tensor_count = lax.axis_size("tp")
    context_count = lax.axis_size("ctx")
    tokens = mixer_input.shape[0]
    channels = mixer_input.shape[1]
    states = state_proj.shape[1] // 2
    heads_local = step_raw.shape[1]
    head_size = channels // heads_local
    taps = conv_weight.shape[0]
    joined = jnp.concatenate([mixer_input, state_proj], axis=1)
    previous = passed_along(joined[tokens - (taps - 1) :], "ctx", 1)
    kernel = jnp.concatenate([conv_weight, conv_state_weight], axis=1)
    filtered = causal_filter(previous.astype(jnp.float32), joined.astype(jnp.float32), kernel)
    values = filtered[:, :channels].reshape(tokens, heads_local, head_size)
    writer = filtered[:, channels : channels + states]
    reader = filtered[:, channels + states :]
    step_size = jax.nn.softplus(step_raw + step_bias[None, :])
    log_decay = -step_size * jnp.exp(decay_log)[None, :]
    inside, cumulative, fresh, tail = local_terms(values, writer, reader, step_size, log_decay)

    incoming = entering(jnp.repeat(jnp.exp(tail), head_size), fresh, "ctx")
    carried = (
        jnp.dot(reader, incoming, precision=lax.Precision.HIGHEST).reshape(values.shape)
        * jnp.exp(cumulative)[:, :, None]
    )
    mixed = inside + carried + skip_gain[None, :, None] * values
    gated = mixed.reshape(tokens, channels) * jax.nn.silu(gate_input.astype(jnp.float32))
    tp_index = lax.axis_index("tp")
    core, chip = (tp_index % 2, tp_index // 2)
    scaled = (gated * mixer_gain[None, :]).astype(jnp.bfloat16)
    direct = context_count == EXPERTS
    ctx_index = lax.axis_index("ctx")
    if direct:
        pairs = []
        for plane in range(4):
            block = rotated(scaled, 2 * plane) if plane else scaled
            other = lax.ppermute(block, "ctx", [(c, c ^ 1) for c in range(context_count)])
            pair = jnp.concatenate([block, other], axis=0)
            pairs.append(jnp.dot(pair, out_weight, preferred_element_type=jnp.float32))
        products = jnp.stack(pairs)

        def projected(quarter):
            place = (ctx_index // 2 - quarter) % 4
            return lax.dynamic_index_in_dim(products, place, 0, keepdims=False)

    else:
        everyone = lax.all_gather(scaled, "ctx", axis=0, tiled=True)
        span = everyone.shape[0] // tensor_count

        def projected(quarter):
            rows = lax.dynamic_slice_in_dim(everyone, quarter * span, span, 0)
            return jnp.dot(rows, out_weight, preferred_element_type=jnp.float32)

    square_sum = tensor_total(jnp.sum(gated * gated, axis=1))
    scale = lax.rsqrt(square_sum / (channels * tensor_count) + EPSILON)
    own, beside = (chip * 2 + core, chip * 2 + 1 - core)
    across, diagonal = ((1 - chip) * 2 + core, (1 - chip) * 2 + 1 - core)
    far = swapped(projected(diagonal).astype(jnp.bfloat16), 1)
    far = swapped((projected(across) + far.astype(jnp.float32)).astype(jnp.bfloat16), 2)
    near = swapped(projected(beside).astype(jnp.bfloat16), 1)
    reduced = projected(own) + near.astype(jnp.float32) + far.astype(jnp.float32)
    blocks = context_count // tensor_count
    reduced = reduced.astype(jnp.bfloat16).reshape(blocks, tokens, -1)
    pieces = []
    for j in range(blocks):
        moves = [
            (c * tensor_count + p, (p * blocks + (c + j) % blocks) * tensor_count + c // blocks)
            for c in range(context_count)
            for p in range(tensor_count)
        ]
        if direct:
            block = reduced[j]
        else:
            block = lax.dynamic_index_in_dim(reduced, (ctx_index + j) % blocks, 0, keepdims=False)
        pieces.append(lax.ppermute(block, ("ctx", "tp"), moves))
    stacked = jnp.stack(pieces)
    order = (ctx_index - jnp.arange(blocks)) % blocks
    if blocks == 2:
        first = ctx_index % 2 == 0
        mixer_out = jnp.concatenate(
            [jnp.where(first, pieces[0], pieces[1]), jnp.where(first, pieces[1], pieces[0])], axis=1
        )
    else:
        mixer_out = jnp.take(stacked, order, axis=0).transpose(1, 0, 2).reshape(tokens, -1)
    mixer_out = mixer_out.astype(jnp.float32) * scale[:, None]
    hidden_state = (residual.astype(jnp.float32) + mixer_out).astype(jnp.bfloat16)
    state_float = lax.optimization_barrier(hidden_state).astype(jnp.float32)
    width_total = hidden_state.shape[1] * tensor_count
    feed_sum = tensor_total(jnp.sum(state_float * state_float, axis=1))
    feed_scale = lax.rsqrt(feed_sum / width_total + EPSILON)
    expert_input = (state_float * feed_scale[:, None] * feed_gain[None, :]).astype(jnp.bfloat16)
    group = context_count // EXPERTS
    width_local = expert_input.shape[1]
    flat_experts = expert_ids.reshape(-1)
    matches = (flat_experts[:, None] == jnp.arange(EXPERTS)[None, :]).astype(jnp.int32)
    slots = jnp.sum((jnp.cumsum(matches, axis=0) - matches) * matches, axis=1)
    places = (flat_experts - ctx_index) % EXPERTS if direct else flat_experts
    targets = (places * CAP + slots).reshape(tokens, -1)
    picker = jnp.any(targets[None, :, :] == jnp.arange(EXPERTS * CAP)[:, None, None], axis=2)
    buffer = jnp.dot(
        picker.astype(jnp.bfloat16), expert_input, preferred_element_type=jnp.float32
    ).astype(jnp.bfloat16)
    outgoing = jnp.broadcast_to(
        buffer.reshape(EXPERTS, 1, CAP, width_local), (EXPERTS, group, CAP, width_local)
    )
    outgoing = outgoing.reshape(EXPERTS * group, CAP, width_local)
    gate_local = expert_gate[0]
    up_local = expert_up[0]
    down_local = expert_down[0]
    sources, items, depth = outgoing.shape
    if direct:
        flattened = jnp.concatenate(
            [outgoing[r] if r == 0 else rotated(outgoing[r], r) for r in range(sources)], axis=0
        )
    else:
        arrived = lax.all_to_all(outgoing, "ctx", split_axis=0, concat_axis=0, tiled=True)
        flattened = arrived.reshape(sources * items, depth)
    hidden = gate_local.shape[1] // tensor_count

    def product(source, weight, quarter):
        columns = lax.dynamic_slice_in_dim(weight, quarter * hidden, hidden, 1)
        return jnp.dot(source, columns, preferred_element_type=jnp.float32)

    fars, nears, rows = ([], [], flattened)
    for weight in (gate_local, up_local):
        far = swapped(product(rows, weight, diagonal).astype(jnp.bfloat16), 1)
        nears.append(swapped(product(rows, weight, beside).astype(jnp.bfloat16), 1))
        far = (product(rows, weight, across) + far.astype(jnp.float32)).astype(jnp.bfloat16)
        far, rows = lax.optimization_barrier((far, rows))
        fars.append(swapped(far, 2))
    gate_share, up_share = (
        product(rows, weight, own).astype(jnp.bfloat16).astype(jnp.float32)
        + near.astype(jnp.float32)
        + far.astype(jnp.float32)
        for weight, near, far in zip((gate_local, up_local), nears, fars)
    )
    share = (jax.nn.silu(gate_share) * up_share).astype(jnp.bfloat16)
    share_across = swapped(share, 2)
    share_beside = swapped(share, 1)
    share_diagonal = swapped(share_across, 1)

    def lowered(part, quarter):
        rows = lax.dynamic_slice_in_dim(down_local, quarter * hidden, hidden, 0)
        return jnp.dot(part, rows, preferred_element_type=jnp.float32)

    answer = (
        lowered(share, own)
        + lowered(share_beside, beside)
        + lowered(share_across, across)
        + lowered(share_diagonal, diagonal)
    ).astype(jnp.bfloat16)
    answer = answer.reshape(sources, items, depth)
    if direct:
        answers = jnp.stack(
            [answer[r] if r == 0 else rotated(answer[r], -r) for r in range(sources)]
        )
    else:
        answers = lax.all_to_all(answer, "ctx", split_axis=0, concat_axis=0, tiled=True)
    summed = jnp.sum(answers.reshape(EXPERTS, group, CAP, width_local), axis=1, dtype=jnp.float32)
    summed = summed.reshape(EXPERTS * CAP, width_local)
    chosen = jnp.take(summed, targets, axis=0)
    routed = jnp.sum(expert_weights[:, :, None] * chosen, axis=1)
    return (state_float + routed).astype(jnp.bfloat16)


def solution(mesh):
    placed = (
        P("ctx", "tp"),
        P("ctx", "tp"),
        P("ctx", "tp"),
        P("ctx", None),
        P("ctx", "tp"),
        P(None, "tp"),
        P(),
        P("tp"),
        P("tp"),
        P("tp"),
        P("tp"),
        P("tp", "ctx"),
        P("tp"),
        P("ctx", "tp", None),
        P("ctx", "tp", None),
        P("ctx", None, "tp"),
        P("ctx", None),
        P("ctx", None),
    )
    return jax.shard_map(
        body, mesh=mesh, in_specs=placed, out_specs=P("ctx", "tp"), check_vma=False
    )
```

```python
import jax
import jax.numpy as jnp
from jax import lax
from jax.sharding import PartitionSpec as P


EXPERTS = 8
CAP = 36


EPSILON = 1e-05


def passed_along(value, axis, steps):
    count = lax.axis_size(axis)
    first, last = (max(0, -steps), min(count, count - steps))
    return lax.ppermute(value, axis, [(source, source + steps) for source in range(first, last)])


def swapped(value, distance):
    return lax.ppermute(value, "tp", [(p, p ^ distance) for p in range(lax.axis_size("tp"))])


def rotated(value, steps):
    count = lax.axis_size("ctx")
    return lax.ppermute(value, "ctx", [(c, (c + steps) % count) for c in range(count)])


def tensor_total(value):
    return (value + swapped(value, 1)) + (swapped(value, 2) + swapped(value, 3))


def entering(decay, fresh, axis):
    peers, position = (lax.axis_size(axis), lax.axis_index(axis))
    packed = jnp.concatenate([fresh, decay[None, :]], axis=0).astype(jnp.bfloat16)
    if peers == EXPERTS:
        total, carry = (jnp.zeros_like(fresh), jnp.ones_like(decay)[None, :])
        for distance in range(1, peers):
            part = passed_along(packed, axis, distance).astype(jnp.float32)
            total = total + carry * part[:-1]
            carry = carry * part[-1:]
        return total
    everything = lax.all_gather(packed, axis).astype(jnp.float32)

    def step(k, before):
        part = everything[k]
        return jnp.where(k < position, part[-1:] * before + part[:-1], before)

    return lax.fori_loop(0, peers, step, jnp.zeros_like(fresh))


def causal_filter(previous, current, kernel):
    joined = jnp.concatenate([previous, current], axis=0)
    length = current.shape[0]
    total = jnp.zeros(current.shape, jnp.float32)
    for offset in range(kernel.shape[0]):
        total = total + kernel[offset][None, :] * joined[offset : offset + length]
    return jax.nn.silu(total)


def local_terms(values, writer, reader, step_size, log_decay):
    length = values.shape[0]
    cumulative = jnp.cumsum(log_decay, axis=0)
    scores = jnp.dot(reader, writer.T, precision=lax.Precision.HIGHEST)
    order = jnp.arange(length)
    causal = (order[:, None] >= order[None, :])[:, :, None]
    spans = cumulative[:, None, :] - cumulative[None, :, :]
    factor = jnp.where(causal, jnp.exp(jnp.where(causal, spans, 0.0)), 0.0)
    factor = factor * step_size[None, :, :] * scores[:, :, None]
    inside = jnp.einsum("tsh,shp->thp", factor, values, precision=lax.Precision.HIGHEST)
    tail = cumulative[length - 1]
    ending = jnp.exp(tail[None, :] - cumulative) * step_size
    weighted = (ending[:, :, None] * values).reshape(length, -1)
    fresh = jnp.dot(writer.T, weighted, precision=lax.Precision.HIGHEST)
    return (inside, cumulative, fresh, tail)


def body(
    residual,
    mixer_input,
    gate_input,
    state_proj,
    step_raw,
    conv_weight,
    conv_state_weight,
    step_bias,
    decay_log,
    skip_gain,
    mixer_gain,
    out_weight,
    feed_gain,
    expert_gate,
    expert_up,
    expert_down,
    expert_ids,
    expert_weights,
):
    tensor_count = lax.axis_size("tp")
    context_count = lax.axis_size("ctx")
    tokens = mixer_input.shape[0]
    channels = mixer_input.shape[1]
    states = state_proj.shape[1] // 2
    heads_local = step_raw.shape[1]
    head_size = channels // heads_local
    taps = conv_weight.shape[0]
    joined = jnp.concatenate([mixer_input, state_proj], axis=1)
    previous = passed_along(joined[tokens - (taps - 1) :], "ctx", 1)
    kernel = jnp.concatenate([conv_weight, conv_state_weight], axis=1)
    filtered = causal_filter(previous.astype(jnp.float32), joined.astype(jnp.float32), kernel)
    values = filtered[:, :channels].reshape(tokens, heads_local, head_size)
    writer = filtered[:, channels : channels + states]
    reader = filtered[:, channels + states :]
    step_size = jax.nn.softplus(step_raw + step_bias[None, :])
    log_decay = -step_size * jnp.exp(decay_log)[None, :]
    inside, cumulative, fresh, tail = local_terms(values, writer, reader, step_size, log_decay)

    incoming = entering(jnp.repeat(jnp.exp(tail), head_size), fresh, "ctx")
    carried = (
        jnp.dot(reader, incoming, precision=lax.Precision.HIGHEST).reshape(values.shape)
        * jnp.exp(cumulative)[:, :, None]
    )
    mixed = inside + carried + skip_gain[None, :, None] * values
    gated = mixed.reshape(tokens, channels) * jax.nn.silu(gate_input.astype(jnp.float32))
    tp_index = lax.axis_index("tp")
    core, chip = (tp_index % 2, tp_index // 2)
    scaled = (gated * mixer_gain[None, :]).astype(jnp.bfloat16)
    direct = context_count == EXPERTS
    ctx_index = lax.axis_index("ctx")
    if direct:
        pairs = []
        for plane in range(4):
            block = rotated(scaled, 2 * plane) if plane else scaled
            other = lax.ppermute(block, "ctx", [(c, c ^ 1) for c in range(context_count)])
            pair = jnp.concatenate([block, other], axis=0)
            pairs.append(jnp.dot(pair, out_weight, preferred_element_type=jnp.float32))
        products = jnp.stack(pairs)

        def projected(quarter):
            place = (ctx_index // 2 - quarter) % 4
            return lax.dynamic_index_in_dim(products, place, 0, keepdims=False)

    else:
        everyone = lax.all_gather(scaled, "ctx", axis=0, tiled=True)
        span = everyone.shape[0] // tensor_count

        def projected(quarter):
            rows = lax.dynamic_slice_in_dim(everyone, quarter * span, span, 0)
            return jnp.dot(rows, out_weight, preferred_element_type=jnp.float32)

    square_sum = tensor_total(jnp.sum(gated * gated, axis=1))
    scale = lax.rsqrt(square_sum / (channels * tensor_count) + EPSILON)
    own, beside = (chip * 2 + core, chip * 2 + 1 - core)
    across, diagonal = ((1 - chip) * 2 + core, (1 - chip) * 2 + 1 - core)
    far = swapped(projected(diagonal).astype(jnp.bfloat16), 1)
    far = swapped((projected(across) + far.astype(jnp.float32)).astype(jnp.bfloat16), 2)
    near = swapped(projected(beside).astype(jnp.bfloat16), 1)
    reduced = projected(own) + near.astype(jnp.float32) + far.astype(jnp.float32)
    blocks = context_count // tensor_count
    reduced = reduced.astype(jnp.bfloat16).reshape(blocks, tokens, -1)
    pieces = []
    for j in range(blocks):
        moves = [
            (c * tensor_count + p, (p * blocks + (c + j) % blocks) * tensor_count + c // blocks)
            for c in range(context_count)
            for p in range(tensor_count)
        ]
        if direct:
            block = reduced[j]
        else:
            block = lax.dynamic_index_in_dim(reduced, (ctx_index + j) % blocks, 0, keepdims=False)
        pieces.append(lax.ppermute(block, ("ctx", "tp"), moves))
    stacked = jnp.stack(pieces)
    order = (ctx_index - jnp.arange(blocks)) % blocks
    if blocks == 2:
        first = ctx_index % 2 == 0
        mixer_out = jnp.concatenate(
            [jnp.where(first, pieces[0], pieces[1]), jnp.where(first, pieces[1], pieces[0])], axis=1
        )
    else:
        mixer_out = jnp.take(stacked, order, axis=0).transpose(1, 0, 2).reshape(tokens, -1)
    mixer_out = mixer_out.astype(jnp.float32) * scale[:, None]
    hidden_state = (residual.astype(jnp.float32) + mixer_out).astype(jnp.bfloat16)
    state_float = lax.optimization_barrier(hidden_state).astype(jnp.float32)
    width_total = hidden_state.shape[1] * tensor_count
    feed_sum = tensor_total(jnp.sum(state_float * state_float, axis=1))
    feed_scale = lax.rsqrt(feed_sum / width_total + EPSILON)
    expert_input = (state_float * feed_scale[:, None] * feed_gain[None, :]).astype(jnp.bfloat16)
    group = context_count // EXPERTS
    width_local = expert_input.shape[1]
    flat_experts = expert_ids.reshape(-1)
    matches = (flat_experts[:, None] == jnp.arange(EXPERTS)[None, :]).astype(jnp.int32)
    slots = jnp.sum((jnp.cumsum(matches, axis=0) - matches) * matches, axis=1)
    places = (flat_experts - ctx_index) % EXPERTS if direct else flat_experts
    targets = (places * CAP + slots).reshape(tokens, -1)
    picker = jnp.any(targets[None, :, :] == jnp.arange(EXPERTS * CAP)[:, None, None], axis=2)
    buffer = jnp.dot(
        picker.astype(jnp.bfloat16), expert_input, preferred_element_type=jnp.float32
    ).astype(jnp.bfloat16)
    outgoing = jnp.broadcast_to(
        buffer.reshape(EXPERTS, 1, CAP, width_local), (EXPERTS, group, CAP, width_local)
    )
    outgoing = outgoing.reshape(EXPERTS * group, CAP, width_local)
    gate_local = expert_gate[0]
    up_local = expert_up[0]
    down_local = expert_down[0]
    sources, items, depth = outgoing.shape
    if direct:
        flattened = jnp.concatenate(
            [outgoing[r] if r == 0 else rotated(outgoing[r], r) for r in range(sources)], axis=0
        )
    else:
        arrived = lax.all_to_all(outgoing, "ctx", split_axis=0, concat_axis=0, tiled=True)
        flattened = arrived.reshape(sources * items, depth)
    hidden = gate_local.shape[1] // tensor_count

    def product(source, weight, quarter):
        columns = lax.dynamic_slice_in_dim(weight, quarter * hidden, hidden, 1)
        return jnp.dot(source, columns, preferred_element_type=jnp.float32)

    fars, nears, rows = ([], [], flattened)
    for weight in (gate_local, up_local):
        far = product(rows, weight, diagonal).astype(jnp.bfloat16)
        far = swapped(far, 1)
        nears.append(swapped(product(rows, weight, beside).astype(jnp.bfloat16), 1))
        far = (product(rows, weight, across) + far.astype(jnp.float32)).astype(jnp.bfloat16)
        far, rows = lax.optimization_barrier((far, rows))
        fars.append(swapped(far, 2))
    gate_share, up_share = (
        product(rows, weight, own).astype(jnp.bfloat16).astype(jnp.float32)
        + near.astype(jnp.float32)
        + far.astype(jnp.float32)
        for weight, near, far in zip((gate_local, up_local), nears, fars)
    )
    share = (jax.nn.silu(gate_share) * up_share).astype(jnp.bfloat16)
    share_across = swapped(share, 2)
    share_beside = swapped(share, 1)

    def lowered(part, quarter):
        rows = lax.dynamic_slice_in_dim(down_local, quarter * hidden, hidden, 0)
        return jnp.dot(part, rows, preferred_element_type=jnp.float32)

    local = lowered(share, own) + lowered(share_beside, beside)
    local, share_across = lax.optimization_barrier((local, share_across))
    share_diagonal = swapped(share_across, 1)
    answer = (
        local
        + lowered(share_across, across)
        + lowered(share_diagonal, diagonal)
    ).astype(jnp.bfloat16)
    answer = answer.reshape(sources, items, depth)
    if direct:
        answers = jnp.stack(
            [answer[r] if r == 0 else rotated(answer[r], -r) for r in range(sources)]
        )
    else:
        answers = lax.all_to_all(answer, "ctx", split_axis=0, concat_axis=0, tiled=True)
    summed = jnp.sum(answers.reshape(EXPERTS, group, CAP, width_local), axis=1, dtype=jnp.float32)
    summed = summed.reshape(EXPERTS * CAP, width_local)
    chosen = jnp.take(summed, targets, axis=0)
    routed = jnp.sum(expert_weights[:, :, None] * chosen, axis=1)
    return (state_float + routed).astype(jnp.bfloat16)


def solution(mesh):
    placed = (
        P("ctx", "tp"),
        P("ctx", "tp"),
        P("ctx", "tp"),
        P("ctx", None),
        P("ctx", "tp"),
        P(None, "tp"),
        P(),
        P("tp"),
        P("tp"),
        P("tp"),
        P("tp"),
        P("tp", "ctx"),
        P("tp"),
        P("ctx", "tp", None),
        P("ctx", "tp", None),
        P("ctx", None, "tp"),
        P("ctx", None),
        P("ctx", None),
    )

    return jax.shard_map(
        body, mesh=mesh, in_specs=placed, out_specs=P("ctx", "tp"), check_vma=False
    )
```

```python
import jax
import jax.numpy as jnp
from jax import lax
from jax.sharding import PartitionSpec as P


EXPERTS = 8
CAP = 36


EPSILON = 1e-05


def passed_along(value, axis, steps):
    count = lax.axis_size(axis)
    first, last = (max(0, -steps), min(count, count - steps))
    return lax.ppermute(value, axis, [(source, source + steps) for source in range(first, last)])


def swapped(value, distance):
    return lax.ppermute(value, "tp", [(p, p ^ distance) for p in range(lax.axis_size("tp"))])


def rotated(value, steps):
    count = lax.axis_size("ctx")
    return lax.ppermute(value, "ctx", [(c, (c + steps) % count) for c in range(count)])


def tensor_total(value):
    return (value + swapped(value, 1)) + (swapped(value, 2) + swapped(value, 3))


def entering(decay, fresh, axis):
    peers, position = (lax.axis_size(axis), lax.axis_index(axis))
    packed = jnp.concatenate([fresh, decay[None, :]], axis=0).astype(jnp.bfloat16)
    if peers == EXPERTS:
        total, carry = (jnp.zeros_like(fresh), jnp.ones_like(decay)[None, :])
        for distance in range(1, peers):
            part = passed_along(packed, axis, distance).astype(jnp.float32)
            total = total + carry * part[:-1]
            carry = carry * part[-1:]
        return total
    everything = lax.all_gather(packed, axis).astype(jnp.float32)

    def step(k, before):
        part = everything[k]
        return jnp.where(k < position, part[-1:] * before + part[:-1], before)

    return lax.fori_loop(0, peers, step, jnp.zeros_like(fresh))


def causal_filter(previous, current, kernel):
    joined = jnp.concatenate([previous, current], axis=0)
    length = current.shape[0]
    total = jnp.zeros(current.shape, jnp.float32)
    for offset in range(kernel.shape[0]):
        total = total + kernel[offset][None, :] * joined[offset : offset + length]
    return jax.nn.silu(total)


def local_terms(values, writer, reader, step_size, log_decay):
    length = values.shape[0]
    cumulative = jnp.cumsum(log_decay, axis=0)
    scores = jnp.dot(reader, writer.T, precision=lax.Precision.HIGHEST)
    order = jnp.arange(length)
    causal = (order[:, None] >= order[None, :])[:, :, None]
    spans = cumulative[:, None, :] - cumulative[None, :, :]
    factor = jnp.where(causal, jnp.exp(jnp.where(causal, spans, 0.0)), 0.0)
    factor = factor * step_size[None, :, :] * scores[:, :, None]
    inside = jnp.einsum("tsh,shp->thp", factor, values, precision=lax.Precision.HIGHEST)
    tail = cumulative[length - 1]
    ending = jnp.exp(tail[None, :] - cumulative) * step_size
    weighted = (ending[:, :, None] * values).reshape(length, -1)
    fresh = jnp.dot(writer.T, weighted, precision=lax.Precision.HIGHEST)
    return (inside, cumulative, fresh, tail)


def body(
    residual,
    mixer_input,
    gate_input,
    state_proj,
    step_raw,
    conv_weight,
    conv_state_weight,
    step_bias,
    decay_log,
    skip_gain,
    mixer_gain,
    out_weight,
    feed_gain,
    expert_gate,
    expert_up,
    expert_down,
    expert_ids,
    expert_weights,
):
    tensor_count = lax.axis_size("tp")
    context_count = lax.axis_size("ctx")
    tokens = mixer_input.shape[0]
    channels = mixer_input.shape[1]
    states = state_proj.shape[1] // 2
    heads_local = step_raw.shape[1]
    head_size = channels // heads_local
    taps = conv_weight.shape[0]
    joined = jnp.concatenate([mixer_input, state_proj], axis=1)
    previous = passed_along(joined[tokens - (taps - 1) :], "ctx", 1)
    kernel = jnp.concatenate([conv_weight, conv_state_weight], axis=1)
    filtered = causal_filter(previous.astype(jnp.float32), joined.astype(jnp.float32), kernel)
    values = filtered[:, :channels].reshape(tokens, heads_local, head_size)
    writer = filtered[:, channels : channels + states]
    reader = filtered[:, channels + states :]
    step_size = jax.nn.softplus(step_raw + step_bias[None, :])
    log_decay = -step_size * jnp.exp(decay_log)[None, :]
    inside, cumulative, fresh, tail = local_terms(values, writer, reader, step_size, log_decay)

    incoming = entering(jnp.repeat(jnp.exp(tail), head_size), fresh, "ctx")
    carried = (
        jnp.dot(reader, incoming, precision=lax.Precision.HIGHEST).reshape(values.shape)
        * jnp.exp(cumulative)[:, :, None]
    )
    mixed = inside + carried + skip_gain[None, :, None] * values
    gated = mixed.reshape(tokens, channels) * jax.nn.silu(gate_input.astype(jnp.float32))
    tp_index = lax.axis_index("tp")
    core, chip = (tp_index % 2, tp_index // 2)
    scaled = (gated * mixer_gain[None, :]).astype(jnp.bfloat16)
    direct = context_count == EXPERTS
    ctx_index = lax.axis_index("ctx")
    if direct:
        pairs = []
        for plane in range(4):
            block = rotated(scaled, 2 * plane) if plane else scaled
            other = lax.ppermute(block, "ctx", [(c, c ^ 1) for c in range(context_count)])
            pair = jnp.concatenate([block, other], axis=0)
            pairs.append(jnp.dot(pair, out_weight, preferred_element_type=jnp.float32))
        products = jnp.stack(pairs)

        def projected(quarter):
            place = (ctx_index // 2 - quarter) % 4
            return lax.dynamic_index_in_dim(products, place, 0, keepdims=False)

    else:
        everyone = lax.all_gather(scaled, "ctx", axis=0, tiled=True)
        span = everyone.shape[0] // tensor_count

        def projected(quarter):
            rows = lax.dynamic_slice_in_dim(everyone, quarter * span, span, 0)
            return jnp.dot(rows, out_weight, preferred_element_type=jnp.float32)

    square_sum = tensor_total(jnp.sum(gated * gated, axis=1))
    scale = lax.rsqrt(square_sum / (channels * tensor_count) + EPSILON)
    own, beside = (chip * 2 + core, chip * 2 + 1 - core)
    across, diagonal = ((1 - chip) * 2 + core, (1 - chip) * 2 + 1 - core)
    far = swapped(projected(diagonal).astype(jnp.bfloat16), 1)
    far = swapped((projected(across) + far.astype(jnp.float32)).astype(jnp.bfloat16), 2)
    near = swapped(projected(beside).astype(jnp.bfloat16), 1)
    reduced = projected(own) + near.astype(jnp.float32) + far.astype(jnp.float32)
    blocks = context_count // tensor_count
    reduced = reduced.astype(jnp.bfloat16).reshape(blocks, tokens, -1)
    pieces = []
    for j in range(blocks):
        moves = [
            (c * tensor_count + p, (p * blocks + (c + j) % blocks) * tensor_count + c // blocks)
            for c in range(context_count)
            for p in range(tensor_count)
        ]
        if direct:
            block = reduced[j]
        else:
            block = lax.dynamic_index_in_dim(reduced, (ctx_index + j) % blocks, 0, keepdims=False)
        pieces.append(lax.ppermute(block, ("ctx", "tp"), moves))
    stacked = jnp.stack(pieces)
    order = (ctx_index - jnp.arange(blocks)) % blocks
    if blocks == 2:
        first = ctx_index % 2 == 0
        mixer_out = jnp.concatenate(
            [jnp.where(first, pieces[0], pieces[1]), jnp.where(first, pieces[1], pieces[0])], axis=1
        )
    else:
        mixer_out = jnp.take(stacked, order, axis=0).transpose(1, 0, 2).reshape(tokens, -1)
    mixer_out = mixer_out.astype(jnp.float32) * scale[:, None]
    hidden_state = (residual.astype(jnp.float32) + mixer_out).astype(jnp.bfloat16)
    state_float = lax.optimization_barrier(hidden_state).astype(jnp.float32)
    width_total = hidden_state.shape[1] * tensor_count
    feed_sum = tensor_total(jnp.sum(state_float * state_float, axis=1))
    feed_scale = lax.rsqrt(feed_sum / width_total + EPSILON)
    expert_input = (state_float * feed_scale[:, None] * feed_gain[None, :]).astype(jnp.bfloat16)
    group = context_count // EXPERTS
    width_local = expert_input.shape[1]
    flat_experts = expert_ids.reshape(-1)
    matches = (flat_experts[:, None] == jnp.arange(EXPERTS)[None, :]).astype(jnp.int32)
    slots = jnp.sum((jnp.cumsum(matches, axis=0) - matches) * matches, axis=1)
    places = (flat_experts - ctx_index) % EXPERTS if direct else flat_experts
    targets = (places * CAP + slots).reshape(tokens, -1)
    picker = jnp.any(targets[None, :, :] == jnp.arange(EXPERTS * CAP)[:, None, None], axis=2)
    buffer = jnp.dot(
        picker.astype(jnp.bfloat16), expert_input, preferred_element_type=jnp.float32
    ).astype(jnp.bfloat16)
    outgoing = jnp.broadcast_to(
        buffer.reshape(EXPERTS, 1, CAP, width_local), (EXPERTS, group, CAP, width_local)
    )
    outgoing = outgoing.reshape(EXPERTS * group, CAP, width_local)
    gate_local = expert_gate[0]
    up_local = expert_up[0]
    down_local = expert_down[0]
    sources, items, depth = outgoing.shape
    if direct:
        flattened = jnp.concatenate(
            [outgoing[r] if r == 0 else rotated(outgoing[r], r) for r in range(sources)], axis=0
        )
    else:
        arrived = lax.all_to_all(outgoing, "ctx", split_axis=0, concat_axis=0, tiled=True)
        flattened = arrived.reshape(sources * items, depth)
    hidden = gate_local.shape[1] // tensor_count

    def product(source, weight, quarter):
        columns = lax.dynamic_slice_in_dim(weight, quarter * hidden, hidden, 1)
        return jnp.dot(source, columns, preferred_element_type=jnp.float32)

    fars, nears, rows = ([], [], flattened)
    for weight in (gate_local, up_local):
        far = product(rows, weight, diagonal).astype(jnp.bfloat16)
        far = swapped(far, 1)
        nears.append(swapped(product(rows, weight, beside).astype(jnp.bfloat16), 1))
        far = (product(rows, weight, across) + far.astype(jnp.float32)).astype(jnp.bfloat16)
        far, rows = lax.optimization_barrier((far, rows))
        fars.append(swapped(far, 2))
    gate_share, up_share = (
        product(rows, weight, own).astype(jnp.bfloat16).astype(jnp.float32)
        + near.astype(jnp.float32)
        + far.astype(jnp.float32)
        for weight, near, far in zip((gate_local, up_local), nears, fars)
    )
    share = (jax.nn.silu(gate_share) * up_share).astype(jnp.bfloat16)
    half = hidden // 2
    arriving = [swapped(share[:, :half], 2)]
    arriving.append(swapped(share[:, half:], 2))
    share_beside = swapped(share, 1)

    def lowered(part, quarter, skipped=0):
        rows = lax.dynamic_slice_in_dim(
            down_local, quarter * hidden + skipped, part.shape[1], 0
        )
        return jnp.dot(part, rows, preferred_element_type=jnp.float32)

    answer = lowered(share, own) + lowered(share_beside, beside)
    for k, part in enumerate(arriving):
        answer, part = lax.optimization_barrier((answer, part))
        forwarded = swapped(part, 1)
        answer = (
            answer
            + lowered(part, across, k * half)
            + lowered(forwarded, diagonal, k * half)
        )
    answer = answer.astype(jnp.bfloat16)
    answer = answer.reshape(sources, items, depth)
    if direct:
        answers = jnp.stack(
            [answer[r] if r == 0 else rotated(answer[r], -r) for r in range(sources)]
        )
    else:
        answers = lax.all_to_all(answer, "ctx", split_axis=0, concat_axis=0, tiled=True)
    summed = jnp.sum(answers.reshape(EXPERTS, group, CAP, width_local), axis=1, dtype=jnp.float32)
    summed = summed.reshape(EXPERTS * CAP, width_local)
    chosen = jnp.take(summed, targets, axis=0)
    routed = jnp.sum(expert_weights[:, :, None] * chosen, axis=1)
    return (state_float + routed).astype(jnp.bfloat16)


def solution(mesh):
    placed = (
        P("ctx", "tp"),
        P("ctx", "tp"),
        P("ctx", "tp"),
        P("ctx", None),
        P("ctx", "tp"),
        P(None, "tp"),
        P(),
        P("tp"),
        P("tp"),
        P("tp"),
        P("tp"),
        P("tp", "ctx"),
        P("tp"),
        P("ctx", "tp", None),
        P("ctx", "tp", None),
        P("ctx", None, "tp"),
        P("ctx", None),
        P("ctx", None),
    )

    return jax.shard_map(
        body, mesh=mesh, in_specs=placed, out_specs=P("ctx", "tp"), check_vma=False
    )
```
